32 devices in a mesh: pb: 2 (over core), pa: 16 (over z, y, x).
Axes of the slice: x: 2, y: 2, z: 4, core: 2. Of those that a mesh axis runs over, the one named last changes fastest.
Arguments:
- queries: bfloat16 [16, 256, 1024], P('pa', 'pb'), may hold values from -25 to 25
- passages: bfloat16 [16, 256, 1024], P('pa', 'pb'), may hold values from -17 to 17
- neighbor_lists: int32 [16, 7], P('pa'), may hold values from -1 to 15, as said below
- positives: int32 [16, 256], P('pa'), may hold values from 0 to 255
- weights: float32 [16, 256], P('pa'), may hold values from 2 to 20
Outputs:
- query_grad: float32 [16, 256, 1024], P('pa', 'pb')
- passage_grad: float32 [16, 256, 1024], P('pa', 'pb')
The draws below stay inside these ranges and needn't reach their ends.
Inputs may be any that keep to these rules, and one draw needn't show every extreme that they name: `neighbor_lists`: row b begins with b; its other entries are distinct blocks within cyclic distance 3 of b, followed by -1 in the remaining slots; some row lists 7 blocks.
All inputs are finite; a program needn't handle non-finite values.
Results may differ from the reference program's by a relative error of at most 0.0045.
Values may be sent and summed in bfloat16 or wider, within the bound.
No kernel may reach another device: no remote copies, remote signals or barrier semaphores. Data moves between devices by JAX's collectives and lax.ppermute only.
A program may use at most 128 MiB of HBM per device.

```python
import math
import jax
import jax.numpy as jnp
from jax import lax

D = 1024
REACH = 3
LIST_MAX = 7
BLOCKS = 16
QB = 256
PBR = 256


def permute_rows(subkey):
    return jax.random.permutation(subkey, PBR)


def embed_pair(key):
    subkeys = jax.random.split(jax.random.fold_in(key, 7), 8)
    passage_scale = jnp.exp(jax.random.uniform(subkeys[0], (BLOCKS, PBR, 1), jnp.float32, jnp.log(0.5), jnp.log(2.0)))
    query_scale = jnp.exp(jax.random.uniform(subkeys[1], (BLOCKS, QB, 1), jnp.float32, jnp.log(0.3), jnp.log(3.0)))
    own_part = jnp.clip(jax.random.normal(subkeys[2], (BLOCKS, PBR, D), jnp.float32), -4.0, 4.0)
    passage_base = own_part
    query_base = jnp.clip(jax.random.normal(subkeys[4], (BLOCKS, QB, D), jnp.float32), -4.0, 4.0)
    passages = passage_base * passage_scale
    unit_rows = own_part / passage_scale
    picks = jax.vmap(permute_rows)(jax.random.split(subkeys[6], BLOCKS * LIST_MAX)).reshape(BLOCKS, LIST_MAX, PBR)
    match_strength = jax.random.uniform(subkeys[7], (BLOCKS, QB, LIST_MAX), jnp.float32, 11.5, 12.5)
    match_factor = match_strength / jnp.sqrt(jnp.float32(D))
    query_slot = jnp.arange(QB, dtype=jnp.int32) % PBR
    own_block = jnp.arange(BLOCKS, dtype=jnp.int32)
    queries = 0.1 * query_base * query_scale
    for slot_number in range(LIST_MAX):
        source_block = (own_block + slot_number - REACH) % BLOCKS
        source_rows = jnp.take(picks[:, slot_number, :], query_slot, axis=1)
        chosen = unit_rows[source_block[:, None], source_rows]
        queries = queries + match_factor[:, :, slot_number:slot_number + 1] * chosen
    return (queries, passages)


def draw_queries(key, part):
    return embed_pair(key)[0].astype(jnp.bfloat16)


def draw_passages(key, part):
    return embed_pair(key)[1].astype(jnp.bfloat16)


def shuffle_one(subkey):
    return jax.random.permutation(subkey, 2 * REACH)


def draw_neighbor_lists(key, part):
    subkeys = jax.random.split(jax.random.fold_in(key, 11), 4)
    half_offsets = jnp.arange(1, REACH + 1, dtype=jnp.int32)
    all_offsets = jnp.concatenate([half_offsets, -half_offsets])
    shuffled = jax.vmap(shuffle_one)(jax.random.split(subkeys[0], BLOCKS))
    chosen_offsets = all_offsets[shuffled]
    list_count = jnp.minimum(jax.random.randint(subkeys[1], (BLOCKS,), 0, 2 * REACH + 1), jax.random.randint(subkeys[2], (BLOCKS,), 0, 2 * REACH + 1))
    full_block = jax.random.randint(subkeys[3], (), 0, BLOCKS)
    own_block = jnp.arange(BLOCKS, dtype=jnp.int32)
    list_count = jnp.where(own_block == full_block, 2 * REACH, list_count)
    neighbor_ids = (own_block[:, None] + chosen_offsets) % BLOCKS
    slot_index = jnp.arange(2 * REACH, dtype=jnp.int32)
    neighbor_ids = jnp.where(slot_index[None, :] < list_count[:, None], neighbor_ids, -1)
    return jnp.concatenate([own_block[:, None], neighbor_ids], axis=1).astype(jnp.int32)


def touch_ends(values, own_key, low, largest):
    longest = values.shape.index(max(values.shape))
    spots = []
    for shift in (0, 1):
        where = [jax.random.randint(jax.random.fold_in(own_key, axis), (), 0, length) for axis, length in enumerate(values.shape)]
        where[longest] = (where[longest] + shift) % values.shape[longest]
        spots.append(tuple(where))
    return values.at[spots[0]].set(low).at[spots[1]].set(largest)


def shard_levels(key, dims, shards, low, high):
    factor_of = 1.0
    for dim, blocks in shards:
        steps = jax.random.uniform(jax.random.fold_in(jax.random.fold_in(key, 6), dim), (blocks,), jnp.float32, low / len(shards), high / len(shards))
        factor_of = factor_of * jnp.repeat(jnp.exp(steps), dims[dim] // blocks).reshape((-1,) + (1,) * (len(dims) - 1 - dim))
    return factor_of


def setup_inputs(seed: int = 0) -> dict:
    keys = jax.random.split(jax.random.key(seed), 6)
    return {
        "queries": draw_queries(jax.random.fold_in(keys[5], 71), 0),
        "passages": draw_passages(jax.random.fold_in(keys[5], 71), 0),
        "neighbor_lists": draw_neighbor_lists(jax.random.fold_in(keys[5], 71), 0),
        "positives": touch_ends(jax.random.randint(keys[3], (BLOCKS, QB), 0, PBR), jax.random.fold_in(keys[3], 1), 0, PBR - 1).astype(jnp.int32),
        "weights": jnp.clip(jnp.exp(math.log(20.0) - 2.3025851 * jax.random.uniform(keys[4], (BLOCKS, QB), jnp.float32) ** shard_levels(keys[4], (BLOCKS, QB), ((0, 16),), -0.2, 0.2)), 2.0, 20.0),
    }


def score_rows(query_rows, block_rows):
    return jnp.dot(query_rows, block_rows.T, preferred_element_type=jnp.float32) * (1.0 / math.sqrt(query_rows.shape[1]))

def empty_rows(query_rows, block_rows):
    return jnp.full((query_rows.shape[0], block_rows.shape[0]), -jnp.inf, jnp.float32)

def multiply_rows(left_side, right_side):
    return jnp.dot(left_side, right_side, preferred_element_type=jnp.float32)

def skip_rows(left_side, right_side):
    return jnp.zeros((left_side.shape[0], right_side.shape[1]), jnp.float32)

def passage_piece(coeff, query_rows):
    return jnp.dot(coeff.T, query_rows, preferred_element_type=jnp.float32).astype(jnp.bfloat16)

def skip_piece(coeff, query_rows):
    return jnp.zeros((coeff.shape[1], query_rows.shape[1]), jnp.bfloat16)

def reference(queries, passages, neighbor_lists, positives, weights):
    score_scale = 1.0 / math.sqrt(D)
    row_index = jnp.arange(PBR, dtype=jnp.int32)

    def one_block(carried, inputs):
        qblock, lists_row, pos_row, weight_row = inputs
        block_ids = jnp.maximum(lists_row, 0).astype(jnp.int32)
        fetched = [lax.dynamic_index_in_dim(passages, block_ids[slot_index], 0, keepdims=False) for slot_index in range(LIST_MAX)]
        is_listed = [lists_row[slot_index] >= 0 for slot_index in range(LIST_MAX)]
        scores = [lax.cond(is_listed[slot_index], score_rows, empty_rows, qblock, fetched[slot_index]) for slot_index in range(LIST_MAX)]
        row_max = lax.optimization_barrier(jnp.max(jnp.stack([lax.optimization_barrier(jnp.max(block_scores, axis=1)) for block_scores in scores]), axis=0))
        row_total = jnp.zeros_like(row_max)
        for block_scores in scores:
            row_total = row_total + lax.optimization_barrier(jnp.sum(jnp.exp(block_scores - row_max[:, None]), axis=1))
        log_total = row_max + jnp.log(row_total)
        onehot = (row_index[None, :] == pos_row[:, None]).astype(jnp.float32)
        query_grad = jnp.zeros((QB, D), jnp.float32)
        for slot_index in range(LIST_MAX):
            probs = jnp.exp(scores[slot_index] - log_total[:, None])
            if slot_index == 0:
                probs = probs - onehot
            coeff = (weight_row[:, None] * probs * score_scale).astype(jnp.bfloat16)
            query_grad = query_grad + lax.cond(is_listed[slot_index], multiply_rows, skip_rows, coeff, fetched[slot_index])
            piece = lax.cond(is_listed[slot_index], passage_piece, skip_piece, coeff, qblock)
            carried = carried.at[block_ids[slot_index]].add(piece.astype(jnp.float32))
        return (carried, query_grad)
    start_grad = jnp.zeros((BLOCKS, PBR, D), jnp.float32)
    passage_grad, query_grad = lax.scan(one_block, start_grad, (queries, neighbor_lists, positives, weights))
    return (query_grad, passage_grad)
```

```python
import math

import jax
import jax.numpy as jnp
from jax import lax
from jax.experimental import pallas as pl
from jax.experimental.pallas import tpu as pltpu
from jax.sharding import PartitionSpec as P

F32 = jnp.float32
BF16 = jnp.bfloat16
WINDOW = 7
LSE_ROW, WEIGHT_ROW, LIST_ROW, STAT_ROWS = 0, 1, 2, 8


def group_shift(i, step, count):
    return (i + step + count) % count


def relay_tables(count):
    every = range(count)
    return {
        "x": [(i, i ^ 1) for i in every],
        "y": [(i, i ^ 2) for i in every],
        "d": [(i, i ^ 3) for i in every],
        "za": [(i, group_shift(i, -4 if i & 2 else 4, count)) for i in every],
        "zb": [(i, group_shift(i, -4 if i & 1 else 4, count)) for i in every],
        "up": [(i, group_shift(i, 4, count)) for i in every],
        "down": [(i, group_shift(i, -4, count)) for i in every],
    }


def window_ids(i, count):
    to_y = jnp.where((i & 2) != 0, 4, -4)
    to_x = jnp.where((i & 1) != 0, 4, -4)
    return [
        i,
        i ^ 1,
        i ^ 2,
        i ^ 3,
        ((i ^ 2) + to_y + count) % count,
        ((i ^ 1) + to_x + count) % count,
        ((i ^ 3) + to_y + count) % count,
    ]


def nt_dot(a, b):
    return lax.dot_general(a, b, (((1,), (1,)), ((), ())), preferred_element_type=F32)


def tn_dot(a, b):
    return lax.dot_general(a, b, (((0,), (0,)), ((), ())), preferred_element_type=F32)


def scores_kernel(count, lists, q_ref, *refs):
    p_refs, (s_ref, ml_ref) = refs[:WINDOW], refs[WINDOW:]
    rows = p_refs[0].shape[0]
    scale = 1.0 / math.sqrt(q_ref.shape[1])
    ids = window_ids(lax.axis_index("pa"), count)
    top = None
    for t in range(WINDOW):
        hit = lists[0, 0] == ids[t]
        for s in range(1, lists.shape[1]):
            hit = jnp.logical_or(hit, lists[0, s] == ids[t])
        bias = jnp.where(hit, 0.0, -jnp.inf).astype(F32)
        part = nt_dot(p_refs[t][...], q_ref[...]) * scale + bias
        s_ref[t * rows : (t + 1) * rows, :] = part
        part_top = jnp.max(part, axis=0, keepdims=True)
        top = part_top if top is None else jnp.maximum(top, part_top)
    total = jnp.zeros_like(top)
    for t in range(WINDOW):
        total += jnp.sum(jnp.exp(s_ref[t * rows : (t + 1) * rows, :] - top), axis=0, keepdims=True)
    ml_ref[...] = jnp.zeros_like(ml_ref)
    ml_ref[0:1, :] = top
    ml_ref[1:2, :] = total


def query_kernel(pb, s_ref, stat_ref, w_ref, pos_ref, *refs):
    p_refs, outs, coeff = refs[:WINDOW], refs[WINDOW:-1], refs[-1]
    rows = p_refs[0].shape[0]
    scale = 1.0 / math.sqrt(p_refs[0].shape[1])
    me = lax.axis_index("pb")
    lse = stat_ref[LSE_ROW : LSE_ROW + 1, :]
    w = w_ref[...]
    row = lax.broadcasted_iota(jnp.int32, (rows, s_ref.shape[1]), 0)
    for t in range(WINDOW):
        prob = jnp.exp(s_ref[t * rows : (t + 1) * rows, :] - lse)
        if t == 0:
            prob = prob - (row == pos_ref[...] - me * rows).astype(F32)
        coeff[t * rows : (t + 1) * rows, :] = (w * prob * scale).astype(BF16)
    for r in range(pb):
        lanes = pl.ds(pl.multiple_of(((me + r) % pb) * rows, rows), rows)
        total = None
        for t in range(WINDOW):
            part = tn_dot(coeff[t * rows : (t + 1) * rows, lanes], p_refs[t][...])
            total = part if total is None else total + part
        outs[r][...] = total.astype(outs[r].dtype)


def cross_kernel(p_ref, *refs):
    q_refs, s_ref = refs[:-1], refs[-1]
    rows = p_ref.shape[0]
    scale = 1.0 / math.sqrt(p_ref.shape[1])
    for n, q_ref in enumerate(q_refs):
        s_ref[:, n * rows : (n + 1) * rows] = nt_dot(p_ref[...], q_ref[...]) * scale


def passage_kernel(pb, s_ref, stat_ref, pos_ref, *refs):
    q_refs, out_ref = refs[:-1], refs[-1]
    rows = out_ref.shape[0]
    scale = 1.0 / math.sqrt(out_ref.shape[1])
    me, home = lax.axis_index("pb"), lax.axis_index("pa").astype(F32)
    row = lax.broadcasted_iota(jnp.int32, (rows, rows), 0)
    total = None
    for t in range(WINDOW):
        lists = stat_ref[t, LIST_ROW : LIST_ROW + 1, :]
        hit = jnp.max(jnp.where(lists == home, 1.0, 0.0), axis=1, keepdims=True) > 0.5
        for r in range(pb):
            n = t * pb + r
            lanes = pl.ds(pl.multiple_of(((me - r + pb) % pb) * rows, rows), rows)
            lse = stat_ref[t, LSE_ROW : LSE_ROW + 1, lanes]
            w = stat_ref[t, WEIGHT_ROW : WEIGHT_ROW + 1, lanes]
            prob = jnp.exp(s_ref[:, n * rows : (n + 1) * rows] - lse)
            if t == 0:
                prob = prob - (row == pos_ref[:, lanes] - me * rows).astype(F32)
            value = jnp.where(hit, w * prob * scale, 0.0).astype(BF16)
            part = jnp.dot(value, q_refs[n][...], preferred_element_type=F32)
            total = part if total is None else total + part
    out_ref[...] = total


VMEM = pl.BlockSpec(memory_space=pltpu.VMEM)
SMEM = pl.BlockSpec(memory_space=pltpu.SMEM)


def call(kernel, outs, specs, args, flops, scratch=()):
    moved = sum(a.size * a.dtype.itemsize for a in (*args, *outs))
    return pl.pallas_call(
        kernel,
        out_shape=outs,
        in_specs=specs,
        out_specs=[VMEM] * len(outs),
        scratch_shapes=list(scratch),
        cost_estimate=pl.CostEstimate(flops=flops, bytes_accessed=moved, transcendentals=0),
        compiler_params=pltpu.CompilerParams(vmem_limit_bytes=32 * 1024 * 1024),
    )(*args)


def body(queries, passages, neighbor_lists, positives, weights):
    pb, count = lax.axis_size("pb"), lax.axis_size("pa")
    own_q, own_p = queries[0], passages[0]
    rows, width = own_p.shape
    q_rows = rows * pb
    tables = relay_tables(count)

    def move(value, name):
        return lax.ppermute(value, "pa", tables[name])

    def from_member(value, by):
        return lax.ppermute(value, "pb", [(i, (i + by) % pb) for i in range(pb)])

    def relay(own):
        x, y = move(own, "x"), move(own, "y")
        za, zb, d = move(y, "za"), move(x, "zb"), move(x, "y")
        return [own, x, y, d, za, zb, move(za, "x")]

    full_q = lax.all_gather(own_q, "pb", axis=0, tiled=True)
    window_p = relay(own_p)
    window_q = relay(own_q)
    flops = 2 * WINDOW * rows * q_rows * width

    def shape(dims, dtype):
        return jax.ShapeDtypeStruct(dims, dtype)

    scores, ml = call(
        lambda *refs: scores_kernel(count, *refs),
        [shape((WINDOW * rows, q_rows), F32), shape((8, q_rows), F32)],
        [SMEM] + [VMEM] * (1 + WINDOW),
        [neighbor_lists, full_q, *window_p],
        flops,
    )
    top, total = ml[0], ml[1]
    for r in range(1, pb):
        other = from_member(ml, r)
        joint = jnp.maximum(top, other[0])
        total = total * jnp.exp(top - joint) + other[1] * jnp.exp(other[0] - joint)
        top = joint
    log_total = top + jnp.log(total)
    lists = jnp.pad(neighbor_lists[0].astype(F32), (0, q_rows - neighbor_lists.shape[1]), constant_values=-1.0)
    stat = jnp.pad(jnp.stack([log_total, weights[0], lists]), ((0, STAT_ROWS - 3), (0, 0)))

    up, down = move(stat, "up"), move(stat, "down")
    trio = jnp.stack([stat, up, down])
    trio_x, trio_y, trio_d = move(trio, "x"), move(trio, "y"), move(trio, "d")
    home = lax.axis_index("pa")
    y_low, x_low = (home & 2) == 0, (home & 1) == 0

    def shifted(trio, low):
        return jnp.where(low, trio[2 - 1], trio[2])

    stats = jnp.stack(
        [stat, trio_x[0], trio_y[0], trio_d[0], shifted(trio_y, y_low), shifted(trio_x, x_low), shifted(trio_d, y_low)]
    )

    parts = call(
        lambda *refs: query_kernel(pb, *refs),
        [shape((rows, width), F32)] + [shape((rows, width), BF16)] * (pb - 1),
        [VMEM] * (4 + WINDOW),
        [scores, stat, weights, positives, *window_p],
        flops,
        [pltpu.VMEM((WINDOW * rows, q_rows), BF16)],
    )
    query_grad = parts[0]
    for r in range(1, pb):
        query_grad = query_grad + from_member(parts[r], r).astype(F32)

    pieces = []
    for block in window_q:
        pieces.append(block)
        for r in range(1, pb):
            pieces.append(from_member(block, r))
    (cross,) = call(
        cross_kernel,
        [shape((rows, WINDOW * q_rows), F32)],
        [VMEM] * (1 + len(pieces)),
        [own_p, *pieces],
        flops,
    )
    (passage_grad,) = call(
        lambda *refs: passage_kernel(pb, *refs),
        [shape((rows, width), F32)],
        [VMEM] * (3 + len(pieces)),
        [cross, stats, positives, *pieces],
        flops,
    )
    return (query_grad[None], passage_grad[None])


def solution(mesh):
    return jax.shard_map(
        body,
        mesh=mesh,
        in_specs=(
            P("pa", "pb", None),
            P("pa", "pb", None),
            P("pa", None),
            P("pa", None),
            P("pa", None),
        ),
        out_specs=(P("pa", "pb", None), P("pa", "pb", None)),
        check_vma=False,
    )
```

```python
import math

import jax
import jax.numpy as jnp
from jax import lax
from jax.experimental import pallas as pl
from jax.experimental.pallas import tpu as pltpu
from jax.sharding import PartitionSpec as P

F32 = jnp.float32
BF16 = jnp.bfloat16
WINDOW = 7
LAST = WINDOW - 1


def group_shift(i, step, count):
    return (i + step + count) % count


def relay_tables(count):
    every = range(count)
    return {
        "x": [(i, i ^ 1) for i in every],
        "y": [(i, i ^ 2) for i in every],
        "d": [(i, i ^ 3) for i in every],
        "za": [(i, group_shift(i, -4 if i & 2 else 4, count)) for i in every],
        "zb": [(i, group_shift(i, -4 if i & 1 else 4, count)) for i in every],
        "up": [(i, group_shift(i, 4, count)) for i in every],
        "down": [(i, group_shift(i, -4, count)) for i in every],
    }


def window_ids(i, count):
    to_y = jnp.where((i & 2) != 0, 4, -4)
    to_x = jnp.where((i & 1) != 0, 4, -4)
    return [
        i,
        i ^ 1,
        i ^ 2,
        i ^ 3,
        ((i ^ 2) + to_y + count) % count,
        ((i ^ 1) + to_x + count) % count,
        ((i ^ 3) + to_y + count) % count,
    ]


def nt_dot(a, b):
    return lax.dot_general(a, b, (((1,), (1,)), ((), ())), preferred_element_type=F32)


def tn_dot(a, b):
    return lax.dot_general(a, b, (((0,), (0,)), ((), ())), preferred_element_type=F32)


def member_slice(member, rows):
    return pl.ds(pl.multiple_of(member * rows, rows), rows)


def fold(part, top, total):
    new_top = jnp.max(part, axis=0, keepdims=True)
    if top is None:
        return new_top, jnp.sum(jnp.exp(part - new_top), axis=0, keepdims=True)
    new_top = jnp.maximum(top, new_top)
    return new_top, total * jnp.exp(top - new_top) + jnp.sum(jnp.exp(part - new_top), axis=0, keepdims=True)


def joined(pairs):
    top = pairs[0][0]
    for other, _ in pairs[1:]:
        top = jnp.maximum(top, other)
    total = jnp.zeros_like(top)
    for other, part in pairs:
        total += part * jnp.exp(other - top)
    return top + jnp.log(total)


def own_kernel(count, pb, lists, w_ref, pos_ref, p_ref, *refs):
    q_refs, (s_ref, ml_ref, full_ref, own_ref, side_ref, where_ref) = refs[:pb], refs[pb:]
    rows, width = p_ref.shape
    scale = 1.0 / math.sqrt(width)
    ids = window_ids(lax.axis_index("pa"), count)
    me = lax.axis_index("pb")
    for r in range(pb):
        full_ref[member_slice((me - r + pb) % pb, rows), :] = q_refs[r][...]
    own_ref[...] = p_ref[...]
    where_ref[...] = pos_ref[...]
    side_ref[...] = jnp.zeros_like(side_ref)
    for t in range(WINDOW):
        hit = lists[0, 0] == ids[t]
        for s in range(1, lists.shape[1]):
            hit = jnp.logical_or(hit, lists[0, s] == ids[t])
        bias = jnp.where(hit, 0.0, -jnp.inf).astype(F32)
        side_ref[t : t + 1, :] = jnp.full((1, side_ref.shape[1]), bias, F32)
    lane = lax.broadcasted_iota(jnp.int32, (1, side_ref.shape[1]), 1)
    listed = jnp.full((1, side_ref.shape[1]), -1.0, F32)
    for s in range(lists.shape[1]):
        listed = jnp.where(lane == s, lists[0, s].astype(F32), listed)
    side_ref[WINDOW : WINDOW + 1, :] = listed
    side_ref[WINDOW + 1 : WINDOW + 2, :] = w_ref[...]
    part = nt_dot(own_ref[...], full_ref[...]) * scale + side_ref[0:1, :]
    s_ref[...] = part
    ml_ref[...] = jnp.zeros_like(ml_ref)
    ml_ref[0:1, :], ml_ref[1:2, :] = fold(part, None, None)


def score_parts(full_ref, side_ref, before_ref, p_refs, s_ref, first):
    rows, width = p_refs[0].shape
    scale = 1.0 / math.sqrt(width)
    before, total = before_ref[0:1, :], before_ref[1:2, :]
    top = before
    for n, p_ref in enumerate(p_refs):
        part = nt_dot(p_ref[...], full_ref[...]) * scale + side_ref[first + n : first + n + 1, :]
        s_ref[n * rows : (n + 1) * rows, :] = part
        top = jnp.maximum(top, jnp.max(part, axis=0, keepdims=True))
    total = total * jnp.exp(before - top)
    for n in range(len(p_refs)):
        total += jnp.sum(jnp.exp(s_ref[n * rows : (n + 1) * rows, :] - top), axis=0, keepdims=True)
    return top, total


def middle_kernel(full_ref, side_ref, before_ref, *refs):
    p_refs, (s_ref, ml_ref) = refs[:-2], refs[-2:]
    ml_ref[...] = jnp.zeros_like(ml_ref)
    ml_ref[0:1, :], ml_ref[1:2, :] = score_parts(full_ref, side_ref, before_ref, p_refs, s_ref, 1)


def last_kernel(pb, full_ref, side_ref, before_ref, p_ref, s_ref, ml_ref, stat_ref):
    top, total = score_parts(full_ref, side_ref, before_ref, [p_ref], s_ref, LAST)
    rows = p_ref.shape[0]
    ml_ref[...] = jnp.zeros_like(ml_ref)
    ml_ref[0:1, :] = top
    ml_ref[1:2, :] = total
    pieces = []
    for value in (top, total, side_ref[WINDOW + 1 : WINDOW + 2, :]):
        pieces += [value[:, c * rows : (c + 1) * rows] for c in range(pb)]
    pieces.append(side_ref[WINDOW : WINDOW + 1, 0:rows])
    stat_ref[...] = jnp.zeros_like(stat_ref)
    stat_ref[0 : len(pieces), :] = jnp.concatenate(pieces, axis=0)


def query_kernel(pb, so_ref, sm_ref, sl_ref, side_ref, pos_ref, *refs):
    ml_refs, p_refs, outs, coeff = refs[:pb], refs[pb : pb + WINDOW], refs[pb + WINDOW : -1], refs[-1]
    rows, width = p_refs[0].shape
    scale = 1.0 / math.sqrt(width)
    me = lax.axis_index("pb")
    lse = joined([(ml[0:1, :], ml[1:2, :]) for ml in ml_refs])
    w = side_ref[WINDOW + 1 : WINDOW + 2, :]
    row = lax.broadcasted_iota(jnp.int32, (rows, w.shape[1]), 0)
    for t in range(WINDOW):
        if t == 0:
            prob = jnp.exp(so_ref[...] - lse) - (row == pos_ref[...] - me * rows).astype(F32)
        elif t == LAST:
            prob = jnp.exp(sl_ref[...] - lse)
        else:
            prob = jnp.exp(sm_ref[(t - 1) * rows : t * rows, :] - lse)
        coeff[t * rows : (t + 1) * rows, :] = (w * prob * scale).astype(BF16)
    for r in range(pb):
        lanes = member_slice((me + r) % pb, rows)
        total = None
        for t in range(WINDOW):
            part = tn_dot(coeff[t * rows : (t + 1) * rows, lanes], p_refs[t][...])
            total = part if total is None else total + part
        outs[r][...] = total.astype(outs[r].dtype)


def cross_kernel(p_ref, *refs):
    q_refs, s_ref = refs[:-1], refs[-1]
    scale = 1.0 / math.sqrt(p_ref.shape[1])
    at = 0
    for q_ref in q_refs:
        s_ref[:, at : at + q_ref.shape[0]] = nt_dot(p_ref[...], q_ref[...]) * scale
        at += q_ref.shape[0]


def passage_kernel(pb, se_ref, sl_ref, pos_ref, *refs):
    grad_refs, stat_refs, refs = refs[:pb], refs[pb : 4 * pb], refs[4 * pb :]
    full_ref, q_refs = refs[0], refs[1 : 1 + pb * LAST]
    out_ref, query_ref, lse_ref, weight_ref = refs[-4:]
    four, up, down = (stat_refs[k * pb : (k + 1) * pb] for k in range(3))
    rows, width = out_ref.shape
    scale = 1.0 / math.sqrt(width)
    grad = grad_refs[0][...]
    for ref in grad_refs[1:]:
        grad = grad + ref[...].astype(F32)
    query_ref[...] = grad
    home, me = lax.axis_index("pa"), lax.axis_index("pb")
    y_low, x_low = (home & 2) == 0, (home & 1) == 0
    row = lax.broadcasted_iota(jnp.int32, (rows, rows), 0)

    def stat(t, c):
        if t < 4:
            return four[c][t]
        k, low = {4: (2, y_low), 5: (1, x_low), 6: (3, y_low)}[t]
        return jnp.where(low, up[c][k], down[c][k])

    total = None
    for t in range(WINDOW):
        mine = [stat(t, c) for c in range(pb)]
        lse_all = joined([(s[0:pb, :], s[pb : 2 * pb, :]) for s in mine])
        w_all = mine[0][2 * pb : 3 * pb, :]
        if t > 0:
            lse_ref[...] = lse_all
            weight_ref[...] = w_all
        hit = jnp.max(jnp.where(mine[0][3 * pb : 3 * pb + 1, :] == home.astype(F32), 1.0, 0.0), axis=1, keepdims=True) > 0.5
        for r in range(pb):
            n = t * pb + r
            if t == 0:
                lse, w, q_block = lse_all[r : r + 1, :], w_all[r : r + 1, :], full_ref[r * rows : (r + 1) * rows, :]
            else:
                member = pl.ds((me - r + pb) % pb, 1)
                lse, w, q_block = lse_ref[member, :], weight_ref[member, :], q_refs[n - pb][...]
            score = se_ref[:, n * rows : (n + 1) * rows] if t < LAST else sl_ref[:, r * rows : (r + 1) * rows]
            prob = jnp.exp(score - lse)
            if t == 0:
                prob = prob - (row == pos_ref[:, r * rows : (r + 1) * rows] - me * rows).astype(F32)
            value = jnp.where(hit, w * prob * scale, 0.0).astype(BF16)
            part = jnp.dot(value, q_block, preferred_element_type=F32)
            total = part if total is None else total + part
    out_ref[...] = total


VMEM = pl.BlockSpec(memory_space=pltpu.VMEM)
SMEM = pl.BlockSpec(memory_space=pltpu.SMEM)


def call(kernel, outs, args, flops, smem=0, scratch=()):
    moved = sum(a.size * a.dtype.itemsize for a in (*args, *outs))
    return pl.pallas_call(
        kernel,
        out_shape=outs,
        in_specs=[SMEM] * smem + [VMEM] * (len(args) - smem),
        out_specs=[VMEM] * len(outs),
        scratch_shapes=list(scratch),
        cost_estimate=pl.CostEstimate(flops=flops, bytes_accessed=moved, transcendentals=0),
        compiler_params=pltpu.CompilerParams(vmem_limit_bytes=24 * 1024 * 1024),
    )(*args)


def shape(dims, dtype):
    return jax.ShapeDtypeStruct(dims, dtype)


def after(value, *others):
    return lax.optimization_barrier((value, *others))[0]


def body(queries, passages, neighbor_lists, positives, weights):
    pb, count = lax.axis_size("pb"), lax.axis_size("pa")
    rows, width = passages.shape[1:]
    q_rows = rows * pb
    tables = relay_tables(count)
    flops = 2 * rows * q_rows * width

    def move(value, name):
        return lax.ppermute(value, "pa", tables[name])

    def from_member(value, r):
        return lax.ppermute(value, "pb", [(i, (i + r) % pb) for i in range(pb)])

    def others(value):
        return [from_member(value, r) for r in range(1, pb)]

    yp, xp = move(passages[0], "y"), move(passages[0], "x")
    yq, xq = move(queries[0], "y"), move(queries[0], "x")
    own_score, own_ml, full_q, own_p, side, where = call(
        lambda *refs: own_kernel(count, pb, *refs),
        [
            shape((rows, q_rows), F32),
            shape((8, q_rows), F32),
            shape((q_rows, width), BF16),
            shape((rows, width), BF16),
            shape((16, q_rows), F32),
            shape((1, q_rows), jnp.int32),
        ],
        [neighbor_lists, weights, positives, passages[0], queries[0], *others(queries[0])],
        flops,
        smem=1,
    )
    zap, zbp, dp = move(yp, "za"), move(xp, "zb"), move(xp, "y")
    xzp = move(after(zap, xq, yq, own_ml), "x")
    middle, middle_ml = call(
        middle_kernel,
        [shape(((LAST - 1) * rows, q_rows), F32), shape((8, q_rows), F32)],
        [full_q, side, own_ml, xp, yp, dp, zap, zbp],
        (LAST - 1) * flops,
    )
    yq2, xq2 = after(yq, zbp), after(xq, zbp)
    zaq, zbq, dq = move(yq2, "za"), move(xq2, "zb"), move(xq2, "y")
    xzq = move(zaq, "x")
    stat_rows = -(-(3 * pb + 1) // 8) * 8
    last, ml, stat = call(
        lambda *refs: last_kernel(pb, *refs),
        [shape((rows, q_rows), F32), shape((8, q_rows), F32), shape((stat_rows, rows), F32)],
        [full_q, side, middle_ml, xzp],
        flops,
    )
    four = jnp.stack([stat, move(stat, "x"), move(stat, "y"), move(stat, "d")])
    up, down = move(four, "up"), move(four, "down")
    parts = call(
        lambda *refs: query_kernel(pb, *refs),
        [shape((rows, width), F32)] + [shape((rows, width), BF16)] * (pb - 1),
        [own_score, middle, last, side, where, ml, *others(ml), own_p, xp, yp, dp, zap, zbp, xzp],
        WINDOW * flops,
        scratch=[pltpu.VMEM((WINDOW * rows, q_rows), BF16)],
    )
    arrived = [from_member(parts[r], r) for r in range(1, pb)]

    pieces = []
    for block in (xq, yq, dq, zaq, zbq, xzq):
        pieces += [block, *others(block)]
    split = (LAST - 1) * pb
    (early_cross,) = call(
        cross_kernel, [shape((rows, LAST * q_rows), F32)], [own_p, full_q, *pieces[:split]], LAST * flops
    )
    (late_cross,) = call(cross_kernel, [shape((rows, q_rows), F32)], [own_p, *pieces[split:]], flops)
    stats = [four, *others(four), up, *others(up), down, *others(down)]
    passage_grad, query_grad = call(
        lambda *refs: passage_kernel(pb, *refs),
        [shape((rows, width), F32)] * 2,
        [early_cross, late_cross, where, parts[0], *arrived, *stats, full_q, *pieces],
        WINDOW * flops,
        scratch=[pltpu.VMEM((pb, rows), F32)] * 2,
    )
    return (query_grad[None], passage_grad[None])


def solution(mesh):
    return jax.shard_map(
        body,
        mesh=mesh,
        in_specs=(
            P("pa", "pb", None),
            P("pa", "pb", None),
            P("pa", None),
            P("pa", None),
            P("pa", None),
        ),
        out_specs=(P("pa", "pb", None), P("pa", "pb", None)),
        check_vma=False,
    )
```

```python
import math

import jax
import jax.numpy as jnp
from jax import lax
from jax.experimental import pallas as pl
from jax.experimental.pallas import tpu as pltpu
from jax.sharding import PartitionSpec as P

F32 = jnp.float32
BF16 = jnp.bfloat16
WINDOW = 7
LAST = WINDOW - 1

def group_shift(i, step, count):
    return (i + step + count) % count

def relay_tables(count):
    every = range(count)
    return {
        "x": [(i, i ^ 1) for i in every],
        "y": [(i, i ^ 2) for i in every],
        "d": [(i, i ^ 3) for i in every],
        "za": [(i, group_shift(i, -4 if i & 2 else 4, count)) for i in every],
        "zb": [(i, group_shift(i, -4 if i & 1 else 4, count)) for i in every],
        "up": [(i, group_shift(i, 4, count)) for i in every],
        "down": [(i, group_shift(i, -4, count)) for i in every],
    }

def window_ids(i, count):
    to_y = jnp.where((i & 2) != 0, 4, -4)
    to_x = jnp.where((i & 1) != 0, 4, -4)
    return [
        i,
        i ^ 1,
        i ^ 2,
        i ^ 3,
        ((i ^ 2) + to_y + count) % count,
        ((i ^ 1) + to_x + count) % count,
        ((i ^ 3) + to_y + count) % count,
    ]

def nt_dot(a, b):
    return lax.dot_general(a, b, (((1,), (1,)), ((), ())), preferred_element_type=F32)

def tn_dot(a, b):
    return lax.dot_general(a, b, (((0,), (0,)), ((), ())), preferred_element_type=F32)

def member_slice(member, rows):
    return pl.ds(pl.multiple_of(member * rows, rows), rows)

def fold(part, top, total):
    new_top = jnp.max(part, axis=0, keepdims=True)
    if top is None:
        return new_top, jnp.sum(jnp.exp(part - new_top), axis=0, keepdims=True)
    new_top = jnp.maximum(top, new_top)
    return new_top, total * jnp.exp(top - new_top) + jnp.sum(jnp.exp(part - new_top), axis=0, keepdims=True)

def joined(pairs):
    top = pairs[0][0]
    for other, _ in pairs[1:]:
        top = jnp.maximum(top, other)
    total = jnp.zeros_like(top)
    for other, part in pairs:
        total += part * jnp.exp(other - top)
    return top + jnp.log(total)

def own_kernel(count, pb, lists, w_ref, pos_ref, p_ref, *refs):
    q_refs, (s_ref, ml_ref, full_ref, own_ref, side_ref, where_ref) = refs[:pb], refs[pb:]
    rows, width = p_ref.shape
    scale = 1.0 / math.sqrt(width)
    ids = window_ids(lax.axis_index("pa"), count)
    me = lax.axis_index("pb")
    for r in range(pb):
        full_ref[member_slice((me - r + pb) % pb, rows), :] = q_refs[r][...]
    own_ref[...] = p_ref[...]
    where_ref[...] = pos_ref[...]
    side_ref[...] = jnp.zeros_like(side_ref)
    for t in range(WINDOW):
        hit = lists[0, 0] == ids[t]
        for s in range(1, lists.shape[1]):
            hit = jnp.logical_or(hit, lists[0, s] == ids[t])
        bias = jnp.where(hit, 0.0, -jnp.inf).astype(F32)
        side_ref[t : t + 1, :] = jnp.full((1, side_ref.shape[1]), bias, F32)
    lane = lax.broadcasted_iota(jnp.int32, (1, side_ref.shape[1]), 1)
    listed = jnp.full((1, side_ref.shape[1]), -1.0, F32)
    for s in range(lists.shape[1]):
        listed = jnp.where(lane == s, lists[0, s].astype(F32), listed)
    side_ref[WINDOW : WINDOW + 1, :] = listed
    side_ref[WINDOW + 1 : WINDOW + 2, :] = w_ref[...]
    part = nt_dot(own_ref[...], full_ref[...]) * scale + side_ref[0:1, :]
    s_ref[...] = part
    ml_ref[...] = jnp.zeros_like(ml_ref)
    ml_ref[0:1, :], ml_ref[1:2, :] = fold(part, None, None)

def score_parts(full_ref, side_ref, before_ref, p_refs, s_ref, first):
    rows, width = p_refs[0].shape
    scale = 1.0 / math.sqrt(width)
    before, total = before_ref[0:1, :], before_ref[1:2, :]
    top = before
    for n, p_ref in enumerate(p_refs):
        part = nt_dot(p_ref[...], full_ref[...]) * scale + side_ref[first + n : first + n + 1, :]
        s_ref[n * rows : (n + 1) * rows, :] = part
        top = jnp.maximum(top, jnp.max(part, axis=0, keepdims=True))
    total = total * jnp.exp(before - top)
    for n in range(len(p_refs)):
        total += jnp.sum(jnp.exp(s_ref[n * rows : (n + 1) * rows, :] - top), axis=0, keepdims=True)
    return top, total

def middle_kernel(full_ref, side_ref, before_ref, *refs):
    p_refs, (s_ref, ml_ref) = refs[:-2], refs[-2:]
    ml_ref[...] = jnp.zeros_like(ml_ref)
    ml_ref[0:1, :], ml_ref[1:2, :] = score_parts(full_ref, side_ref, before_ref, p_refs, s_ref, 1)

def last_kernel(pb, full_ref, side_ref, before_ref, p_ref, s_ref, stat_ref):
    top, total = score_parts(full_ref, side_ref, before_ref, [p_ref], s_ref, LAST)
    rows = p_ref.shape[0]
    pieces = []
    for value in (top, total, side_ref[WINDOW + 1 : WINDOW + 2, :]):
        pieces += [value[:, c * rows : (c + 1) * rows] for c in range(pb)]
    pieces.append(side_ref[WINDOW : WINDOW + 1, 0:rows])
    stat_ref[...] = jnp.zeros_like(stat_ref)
    stat_ref[0 : len(pieces), :] = jnp.concatenate(pieces, axis=0)

def log_totals(stats, pb):
    return joined([(stat[0:pb, :], stat[pb : 2 * pb, :]) for stat in stats])

def query_kernel(pb, so_ref, sm_ref, sl_ref, side_ref, pos_ref, *refs):
    stat_refs, p_refs, outs, coeff = refs[:pb], refs[pb : pb + WINDOW], refs[pb + WINDOW : -1], refs[-1]
    rows, width = p_refs[0].shape
    scale = 1.0 / math.sqrt(width)
    me = lax.axis_index("pb")
    lse_rows = log_totals([ref[0] for ref in stat_refs], pb)
    lse = jnp.concatenate([lse_rows[c : c + 1, :] for c in range(pb)], axis=1)
    w = side_ref[WINDOW + 1 : WINDOW + 2, :]
    row = lax.broadcasted_iota(jnp.int32, (rows, w.shape[1]), 0)
    for t in range(WINDOW):
        if t == 0:
            prob = jnp.exp(so_ref[...] - lse) - (row == pos_ref[...] - me * rows).astype(F32)
        elif t == LAST:
            prob = jnp.exp(sl_ref[...] - lse)
        else:
            prob = jnp.exp(sm_ref[(t - 1) * rows : t * rows, :] - lse)
        coeff[t * rows : (t + 1) * rows, :] = (w * prob * scale).astype(BF16)
    for r in range(pb):
        lanes = member_slice((me + r) % pb, rows)
        total = None
        for t in range(WINDOW):
            part = tn_dot(coeff[t * rows : (t + 1) * rows, lanes], p_refs[t][...])
            total = part if total is None else total + part
        outs[r][...] = total.astype(outs[r].dtype)

def add_blocks(pb, stats, scores, pieces, orders, keep, corrections, total):
    lse_ref, weight_ref = keep
    home = lax.axis_index("pa").astype(F32)
    rows, width = pieces[0].shape
    scale = 1.0 / math.sqrt(width)
    for t, mine in enumerate(stats):
        lse_ref[t] = log_totals(mine, pb)
        weight_ref[t] = mine[0][2 * pb : 3 * pb, :]
        hit = jnp.max(jnp.where(mine[0][3 * pb : 3 * pb + 1, :] == home, 1.0, 0.0), axis=1, keepdims=True) > 0.5
        for r in range(pb):
            n = t * pb + r
            member = pl.ds(orders[n], 1)
            prob = jnp.exp(scores(n) - lse_ref[t, member, :])
            if n in corrections:
                prob = prob - corrections[n]
            value = jnp.where(hit, weight_ref[t, member, :] * prob * scale, 0.0).astype(BF16)
            part = jnp.dot(value, pieces[n][...], preferred_element_type=F32)
            total = part if total is None else total + part
    return total

def near_kernel(pb, p_ref, pos_ref, *refs):
    stat_refs, q_refs = refs[:pb], refs[pb : -4]
    out_ref, s_ref, keep = refs[-4], refs[-3], refs[-2:]
    rows, width = p_ref.shape
    scale = 1.0 / math.sqrt(width)
    me = lax.axis_index("pb")
    row = lax.broadcasted_iota(jnp.int32, (rows, rows), 0)
    full_ref = q_refs[0]
    pieces = [full_ref.at[r * rows : (r + 1) * rows, :] for r in range(pb)] + list(q_refs[1:])
    orders = list(range(pb)) + [(me - r + pb) % pb for _ in range(3) for r in range(pb)]
    corrections = {
        r: (row == pos_ref[:, r * rows : (r + 1) * rows] - me * rows).astype(F32) for r in range(pb)
    }
    for n, piece in enumerate(pieces):
        s_ref[:, n * rows : (n + 1) * rows] = nt_dot(p_ref[...], piece[...]) * scale
    stats = [[ref[t] for ref in stat_refs] for t in range(4)]
    out_ref[...] = add_blocks(
        pb, stats, lambda n: s_ref[:, n * rows : (n + 1) * rows], pieces, orders, keep, corrections, None
    )

def cross_kernel(p_ref, *refs):
    q_refs, s_ref = refs[:-1], refs[-1]
    rows, width = p_ref.shape
    scale = 1.0 / math.sqrt(width)
    for n, q_ref in enumerate(q_refs):
        s_ref[:, n * rows : (n + 1) * rows] = nt_dot(p_ref[...], q_ref[...]) * scale

def far_kernel(pb, s_ref, near_ref, *refs):
    grad_refs, up, down = refs[:pb], refs[pb : 2 * pb], refs[2 * pb : 3 * pb]
    q_refs, (out_ref, query_ref), keep = refs[3 * pb : 6 * pb], refs[6 * pb : 6 * pb + 2], refs[6 * pb + 2 :]
    rows = out_ref.shape[0]
    home, me = lax.axis_index("pa"), lax.axis_index("pb")
    y_low, x_low = (home & 2) == 0, (home & 1) == 0
    stats = []
    for k, low in ((2, y_low), (1, x_low), (3, y_low)):
        stats.append([jnp.where(low, up[c][k], down[c][k]) for c in range(pb)])
    orders = [(me - r + pb) % pb for _ in range(3) for r in range(pb)]
    out_ref[...] = add_blocks(
        pb, stats, lambda n: s_ref[:, n * rows : (n + 1) * rows], q_refs, orders, keep, {}, near_ref[...]
    )
    grad = grad_refs[0][...]
    for ref in grad_refs[1:]:
        grad = grad + ref[...].astype(F32)
    query_ref[...] = grad

VMEM = pl.BlockSpec(memory_space=pltpu.VMEM)
SMEM = pl.BlockSpec(memory_space=pltpu.SMEM)

def call(kernel, outs, args, flops, smem=0, scratch=()):
    return pl.pallas_call(
        kernel,
        out_shape=outs,
        in_specs=[SMEM] * smem + [VMEM] * (len(args) - smem),
        out_specs=[VMEM] * len(outs),
        scratch_shapes=list(scratch),
        cost_estimate=pl.CostEstimate(flops=0, bytes_accessed=0, transcendentals=0),
        compiler_params=pltpu.CompilerParams(vmem_limit_bytes=24 * 1024 * 1024),
    )(*args)

def shape(dims, dtype):
    return jax.ShapeDtypeStruct(dims, dtype)

def after(value, *others):
    return lax.optimization_barrier((value, *others))[0]

def body(queries, passages, neighbor_lists, positives, weights):
    pb, count = lax.axis_size("pb"), lax.axis_size("pa")
    rows, width = passages.shape[1:]
    q_rows = rows * pb
    tables = relay_tables(count)
    flops = 2 * rows * q_rows * width

    def move(value, name):
        return lax.ppermute(value, "pa", tables[name])

    def from_member(value, r):
        return lax.ppermute(value, "pb", [(i, (i + r) % pb) for i in range(pb)])

    def others(value):
        return [from_member(value, r) for r in range(1, pb)]

    yp, xp = move(passages[0], "y"), move(passages[0], "x")
    yq, xq = move(queries[0], "y"), move(queries[0], "x")
    own_score, own_ml, full_q, own_p, side, where = call(
        lambda *refs: own_kernel(count, pb, *refs),
        [
            shape((rows, q_rows), F32),
            shape((8, q_rows), F32),
            shape((q_rows, width), BF16),
            shape((rows, width), BF16),
            shape((16, q_rows), F32),
            shape((1, q_rows), jnp.int32),
        ],
        [neighbor_lists, weights, positives, passages[0], queries[0], *others(queries[0])],
        flops,
        smem=1,
    )
    xqs, yqs = [xq, *others(xq)], [yq, *others(yq)]
    zap, zbp, dp = move(yp, "za"), move(xp, "zb"), move(xp, "y")
    xzp = move(after(zap, xq, yq, own_ml), "x")
    middle, middle_ml = call(
        middle_kernel,
        [shape(((LAST - 1) * rows, q_rows), F32), shape((8, q_rows), F32)],
        [full_q, side, after(own_ml, *xqs, *yqs), xp, yp, dp, zap, zbp],
        (LAST - 1) * flops,
    )
    zaq, zbq = move(after(yq, zbp), "za"), move(after(xq, zbp), "zb")
    stat_rows = -(-(3 * pb + 1) // 8) * 8
    last, stat = call(
        lambda *refs: last_kernel(pb, *refs),
        [shape((rows, q_rows), F32), shape((stat_rows, rows), F32)],
        [full_q, side, middle_ml, xzp],
        flops,
    )
    stat_x, stat_y, stat_d = move(stat, "x"), move(stat, "y"), move(stat, "d")
    four = jnp.stack([stat, stat_x, stat_y, stat_d])
    dq = move(after(xq, four), "y")
    xzq = move(after(zaq, four), "x")
    up, down = move(four, "up"), move(four, "down")
    fours = [four, *others(four)]
    parts = call(
        lambda *refs: query_kernel(pb, *refs),
        [shape((rows, width), F32)] + [shape((rows, width), BF16)] * (pb - 1),
        [own_score, middle, last, side, where, *fours, own_p, xp, yp, dp, zap, zbp, xzp],
        WINDOW * flops,
        scratch=[pltpu.VMEM((WINDOW * rows, q_rows), BF16)],
    )
    arrived = [from_member(parts[r], r) for r in range(1, pb)]

    def keep(blocks):
        return [pltpu.VMEM((blocks, pb, rows), F32)] * 2

    (near,) = call(
        lambda *refs: near_kernel(pb, *refs),
        [shape((rows, width), F32)],
        [own_p, where, *fours, full_q, *xqs, *yqs, dq, *others(dq)],
        8 * flops,
        scratch=[pltpu.VMEM((rows, 4 * q_rows), F32), *keep(4)],
    )
    far_q = [zaq, *others(after(zaq, dq)), zbq, *others(after(zbq, dq)), xzq, *others(xzq)]
    (cross,) = call(cross_kernel, [shape((rows, 3 * q_rows), F32)], [own_p, *far_q], 3 * flops)
    passage_grad, query_grad = call(
        lambda *refs: far_kernel(pb, *refs),
        [shape((rows, width), F32)] * 2,
        [cross, near, parts[0], *arrived, up, *others(up), down, *others(down), *far_q],
        3 * flops,
        scratch=keep(3),
    )
    return (query_grad[None], passage_grad[None])

def solution(mesh):
    return jax.shard_map(
        body,
        mesh=mesh,
        in_specs=(
            P("pa", "pb", None),
            P("pa", "pb", None),
            P("pa", None),
            P("pa", None),
            P("pa", None),
        ),
        out_specs=(P("pa", "pb", None), P("pa", "pb", None)),
        check_vma=False,
    )
```

```python
import math

import jax
import jax.numpy as jnp
from jax import lax
from jax.experimental import pallas as pl
from jax.experimental.pallas import tpu as pltpu
from jax.sharding import PartitionSpec as P

F32 = jnp.float32
BF16 = jnp.bfloat16
WINDOW = 7
LAST = WINDOW - 1

def group_shift(i, step, count):
    return (i + step + count) % count

def relay_tables(count):
    every = range(count)
    return {
        "x": [(i, i ^ 1) for i in every],
        "y": [(i, i ^ 2) for i in every],
        "d": [(i, i ^ 3) for i in every],
        "za": [(i, group_shift(i, -4 if i & 2 else 4, count)) for i in every],
        "zb": [(i, group_shift(i, -4 if i & 1 else 4, count)) for i in every],
        "up": [(i, group_shift(i, 4, count)) for i in every],
        "down": [(i, group_shift(i, -4, count)) for i in every],
    }

def window_ids(i, count):
    to_y = jnp.where((i & 2) != 0, 4, -4)
    to_x = jnp.where((i & 1) != 0, 4, -4)
    return [
        i,
        i ^ 1,
        i ^ 2,
        i ^ 3,
        ((i ^ 2) + to_y + count) % count,
        ((i ^ 1) + to_x + count) % count,
        ((i ^ 3) + to_y + count) % count,
    ]

def nt_dot(a, b):
    return lax.dot_general(a, b, (((1,), (1,)), ((), ())), preferred_element_type=F32)

def tn_dot(a, b):
    return lax.dot_general(a, b, (((0,), (0,)), ((), ())), preferred_element_type=F32)

def member_slice(member, rows):
    return pl.ds(pl.multiple_of(member * rows, rows), rows)

def fold(part, top, total):
    new_top = jnp.max(part, axis=0, keepdims=True)
    if top is None:
        return new_top, jnp.sum(jnp.exp(part - new_top), axis=0, keepdims=True)
    new_top = jnp.maximum(top, new_top)
    return new_top, total * jnp.exp(top - new_top) + jnp.sum(jnp.exp(part - new_top), axis=0, keepdims=True)

def joined(pairs):
    top = pairs[0][0]
    for other, _ in pairs[1:]:
        top = jnp.maximum(top, other)
    total = jnp.zeros_like(top)
    for other, part in pairs:
        total += part * jnp.exp(other - top)
    return top + jnp.log(total)

def own_kernel(count, pb, lists, w_ref, pos_ref, p_ref, *refs):
    q_refs, (s_ref, ml_ref, full_ref, own_ref, side_ref, where_ref) = refs[:pb], refs[pb:]
    rows, width = p_ref.shape
    scale = 1.0 / math.sqrt(width)
    ids = window_ids(lax.axis_index("pa"), count)
    me = lax.axis_index("pb")
    for r in range(pb):
        full_ref[member_slice((me - r + pb) % pb, rows), :] = q_refs[r][...]
    own_ref[...] = p_ref[...]
    where_ref[...] = pos_ref[...]
    side_ref[...] = jnp.zeros_like(side_ref)
    for t in range(WINDOW):
        hit = lists[0, 0] == ids[t]
        for s in range(1, lists.shape[1]):
            hit = jnp.logical_or(hit, lists[0, s] == ids[t])
        bias = jnp.where(hit, 0.0, -jnp.inf).astype(F32)
        side_ref[t : t + 1, :] = jnp.full((1, side_ref.shape[1]), bias, F32)
    lane = lax.broadcasted_iota(jnp.int32, (1, side_ref.shape[1]), 1)
    listed = jnp.full((1, side_ref.shape[1]), -1.0, F32)
    for s in range(lists.shape[1]):
        listed = jnp.where(lane == s, lists[0, s].astype(F32), listed)
    side_ref[WINDOW : WINDOW + 1, :] = listed
    side_ref[WINDOW + 1 : WINDOW + 2, :] = w_ref[...]
    part = nt_dot(own_ref[...], full_ref[...]) * scale + side_ref[0:1, :]
    s_ref[...] = part
    ml_ref[...] = jnp.zeros_like(ml_ref)
    ml_ref[0:1, :], ml_ref[1:2, :] = fold(part, None, None)

def score_parts(full_ref, side_ref, before_ref, p_refs, s_ref, first):
    rows, width = p_refs[0].shape
    scale = 1.0 / math.sqrt(width)
    before, total = before_ref[0:1, :], before_ref[1:2, :]
    top = before
    for n, p_ref in enumerate(p_refs):
        part = nt_dot(p_ref[...], full_ref[...]) * scale + side_ref[first + n : first + n + 1, :]
        s_ref[n * rows : (n + 1) * rows, :] = part
        top = jnp.maximum(top, jnp.max(part, axis=0, keepdims=True))
    total = total * jnp.exp(before - top)
    for n in range(len(p_refs)):
        total += jnp.sum(jnp.exp(s_ref[n * rows : (n + 1) * rows, :] - top), axis=0, keepdims=True)
    return top, total

def middle_kernel(full_ref, side_ref, before_ref, *refs):
    p_refs, (s_ref, ml_ref) = refs[:-2], refs[-2:]
    ml_ref[...] = jnp.zeros_like(ml_ref)
    ml_ref[0:1, :], ml_ref[1:2, :] = score_parts(full_ref, side_ref, before_ref, p_refs, s_ref, 1)

def last_kernel(pb, full_ref, side_ref, before_ref, p_ref, s_ref, stat_ref):
    top, total = score_parts(full_ref, side_ref, before_ref, [p_ref], s_ref, LAST)
    rows = p_ref.shape[0]
    pieces = []
    for value in (top, total, side_ref[WINDOW + 1 : WINDOW + 2, :]):
        pieces += [value[:, c * rows : (c + 1) * rows] for c in range(pb)]
    pieces.append(side_ref[WINDOW : WINDOW + 1, 0:rows])
    stat_ref[...] = jnp.zeros_like(stat_ref)
    stat_ref[0 : len(pieces), :] = jnp.concatenate(pieces, axis=0)

def log_totals(stats, pb):
    return joined([(stat[0:pb, :], stat[pb : 2 * pb, :]) for stat in stats])

def query_kernel(pb, so_ref, sm_ref, sl_ref, side_ref, pos_ref, *refs):
    stat_refs, p_refs, outs, coeff = refs[:pb], refs[pb : pb + WINDOW], refs[pb + WINDOW : -1], refs[-1]
    rows, width = p_refs[0].shape
    scale = 1.0 / math.sqrt(width)
    me = lax.axis_index("pb")
    lse_rows = log_totals([ref[0] for ref in stat_refs], pb)
    lse = jnp.concatenate([lse_rows[c : c + 1, :] for c in range(pb)], axis=1)
    w = side_ref[WINDOW + 1 : WINDOW + 2, :]
    row = lax.broadcasted_iota(jnp.int32, (rows, w.shape[1]), 0)
    for t in range(WINDOW):
        if t == 0:
            prob = jnp.exp(so_ref[...] - lse) - (row == pos_ref[...] - me * rows).astype(F32)
        elif t == LAST:
            prob = jnp.exp(sl_ref[...] - lse)
        else:
            prob = jnp.exp(sm_ref[(t - 1) * rows : t * rows, :] - lse)
        coeff[t * rows : (t + 1) * rows, :] = (w * prob * scale).astype(BF16)
    for r in range(pb):
        lanes = member_slice((me + r) % pb, rows)
        total = None
        for t in range(WINDOW):
            part = tn_dot(coeff[t * rows : (t + 1) * rows, lanes], p_refs[t][...])
            total = part if total is None else total + part
        outs[r][...] = total.astype(outs[r].dtype)

def add_blocks(pb, stats, scores, pieces, orders, keep, corrections, total):
    lse_ref, weight_ref = keep
    home = lax.axis_index("pa").astype(F32)
    rows, width = pieces[0].shape
    scale = 1.0 / math.sqrt(width)
    for t, mine in enumerate(stats):
        lse_ref[t] = log_totals(mine, pb)
        weight_ref[t] = mine[0][2 * pb : 3 * pb, :]
        hit = jnp.max(jnp.where(mine[0][3 * pb : 3 * pb + 1, :] == home, 1.0, 0.0), axis=1, keepdims=True) > 0.5
        for r in range(pb):
            n = t * pb + r
            member = pl.ds(orders[n], 1)
            prob = jnp.exp(scores(n) - lse_ref[t, member, :])
            if n in corrections:
                prob = prob - corrections[n]
            value = jnp.where(hit, weight_ref[t, member, :] * prob * scale, 0.0).astype(BF16)
            part = jnp.dot(value, pieces[n][...], preferred_element_type=F32)
            total = part if total is None else total + part
    return total

def near_kernel(pb, p_ref, pos_ref, *refs):
    stat_refs, q_refs = refs[:pb], refs[pb : -4]
    out_ref, s_ref, keep = refs[-4], refs[-3], refs[-2:]
    rows, width = p_ref.shape
    scale = 1.0 / math.sqrt(width)
    me = lax.axis_index("pb")
    row = lax.broadcasted_iota(jnp.int32, (rows, rows), 0)
    full_ref = q_refs[0]
    pieces = [full_ref.at[r * rows : (r + 1) * rows, :] for r in range(pb)] + list(q_refs[1:])
    orders = list(range(pb)) + [(me - r + pb) % pb for _ in range(3) for r in range(pb)]
    corrections = {
        r: (row == pos_ref[:, r * rows : (r + 1) * rows] - me * rows).astype(F32) for r in range(pb)
    }
    for n, piece in enumerate(pieces):
        s_ref[:, n * rows : (n + 1) * rows] = nt_dot(p_ref[...], piece[...]) * scale
    stats = [[ref[t] for ref in stat_refs] for t in range(4)]
    out_ref[...] = add_blocks(
        pb, stats, lambda n: s_ref[:, n * rows : (n + 1) * rows], pieces, orders, keep, corrections, None
    )

def cross_kernel(p_ref, *refs):
    q_refs, s_ref = refs[:-1], refs[-1]
    rows, width = p_ref.shape
    scale = 1.0 / math.sqrt(width)
    for n, q_ref in enumerate(q_refs):
        s_ref[:, n * rows : (n + 1) * rows] = nt_dot(p_ref[...], q_ref[...]) * scale

def far_kernel(pb, s_ref, near_ref, *refs):
    grad_refs, up, down = refs[:pb], refs[pb : 2 * pb], refs[2 * pb : 3 * pb]
    q_refs, (out_ref, query_ref), keep = refs[3 * pb : 6 * pb], refs[6 * pb : 6 * pb + 2], refs[6 * pb + 2 :]
    rows = out_ref.shape[0]
    home, me = lax.axis_index("pa"), lax.axis_index("pb")
    y_low, x_low = (home & 2) == 0, (home & 1) == 0
    stats = []
    for k, low in ((2, y_low), (1, x_low), (3, y_low)):
        stats.append([jnp.where(low, up[c][k], down[c][k]) for c in range(pb)])
    orders = [(me - r + pb) % pb for _ in range(3) for r in range(pb)]
    out_ref[...] = add_blocks(
        pb, stats, lambda n: s_ref[:, n * rows : (n + 1) * rows], q_refs, orders, keep, {}, near_ref[...]
    )
    grad = grad_refs[0][...]
    for ref in grad_refs[1:]:
        grad = grad + ref[...].astype(F32)
    query_ref[...] = grad

VMEM = pl.BlockSpec(memory_space=pltpu.VMEM)
SMEM = pl.BlockSpec(memory_space=pltpu.SMEM)

def call(kernel, outs, args, flops, smem=0, scratch=()):
    return pl.pallas_call(
        kernel,
        out_shape=outs,
        in_specs=[SMEM] * smem + [VMEM] * (len(args) - smem),
        out_specs=[VMEM] * len(outs),
        scratch_shapes=list(scratch),
        cost_estimate=pl.CostEstimate(flops=0, bytes_accessed=0, transcendentals=0),
        compiler_params=pltpu.CompilerParams(vmem_limit_bytes=24 * 1024 * 1024),
    )(*args)

def shape(dims, dtype):
    return jax.ShapeDtypeStruct(dims, dtype)

def after(value, *others):
    return lax.optimization_barrier((value, *others))[0]

def body(queries, passages, neighbor_lists, positives, weights):
    pb, count = lax.axis_size("pb"), lax.axis_size("pa")
    rows, width = passages.shape[1:]
    q_rows = rows * pb
    tables = relay_tables(count)
    flops = 2 * rows * q_rows * width

    def move(value, name):
        return lax.ppermute(value, "pa", tables[name])

    def from_member(value, r):
        return lax.ppermute(value, "pb", [(i, (i + r) % pb) for i in range(pb)])

    def others(value):
        return [from_member(value, r) for r in range(1, pb)]

    yp, xp = move(passages[0], "y"), move(passages[0], "x")
    yq, xq = move(queries[0], "y"), move(queries[0], "x")
    own_score, own_ml, full_q, own_p, side, where = call(
        lambda *refs: own_kernel(count, pb, *refs),
        [
            shape((rows, q_rows), F32),
            shape((8, q_rows), F32),
            shape((q_rows, width), BF16),
            shape((rows, width), BF16),
            shape((16, q_rows), F32),
            shape((1, q_rows), jnp.int32),
        ],
        [neighbor_lists, weights, positives, passages[0], queries[0], *others(queries[0])],
        flops,
        smem=1,
    )
    xqs, yqs = [xq, *others(xq)], [yq, *others(yq)]
    zap, dp = move(yp, "za"), move(xp, "y")
    zbp = move(xp, "zb")
    xzp = move(after(zap, xq, yq, own_ml), "x")
    middle, middle_ml = call(
        middle_kernel,
        [shape(((LAST - 1) * rows, q_rows), F32), shape((8, q_rows), F32)],
        [full_q, side, own_ml, xp, yp, dp, zap, zbp],
        (LAST - 1) * flops,
    )
    zaq = move(after(yq, zbp), "za")
    zbq = move(after(xq, zbp), "zb")
    dq = move(after(xq, xzp), "y")
    stat_rows = -(-(3 * pb + 1) // 8) * 8
    last, stat = call(
        lambda *refs: last_kernel(pb, *refs),
        [shape((rows, q_rows), F32), shape((stat_rows, rows), F32)],
        [full_q, side, middle_ml, xzp],
        flops,
    )
    stat_x = move(stat, "x")
    stat_y = move(stat, "y")
    stat_d = move(stat, "d")
    four = jnp.stack([after(stat, *xqs, *yqs), stat_x, stat_y, stat_d])
    xzq = move(after(zaq, four), "x")
    up, down = move(four, "up"), move(four, "down")
    fours = [four, *others(four)]
    parts = call(
        lambda *refs: query_kernel(pb, *refs),
        [shape((rows, width), F32)] + [shape((rows, width), BF16)] * (pb - 1),
        [own_score, middle, last, side, where, *fours, own_p, xp, yp, dp, zap, zbp, xzp],
        WINDOW * flops,
        scratch=[pltpu.VMEM((WINDOW * rows, q_rows), BF16)],
    )
    arrived = [from_member(parts[r], r) for r in range(1, pb)]

    def keep(blocks):
        return [pltpu.VMEM((blocks, pb, rows), F32)] * 2

    (near,) = call(
        lambda *refs: near_kernel(pb, *refs),
        [shape((rows, width), F32)],
        [own_p, where, *fours, full_q, *xqs, *yqs, dq, *others(after(dq, parts[0]))],
        8 * flops,
        scratch=[pltpu.VMEM((rows, 4 * q_rows), F32), *keep(4)],
    )
    far_q = [zaq, *others(after(zaq, dq)), zbq, *others(after(zbq, dq)), xzq, *others(xzq)]
    (cross,) = call(cross_kernel, [shape((rows, 3 * q_rows), F32)], [own_p, *far_q], 3 * flops)
    passage_grad, query_grad = call(
        lambda *refs: far_kernel(pb, *refs),
        [shape((rows, width), F32)] * 2,
        [cross, near, parts[0], *arrived, up, *others(up), down, *others(down), *far_q],
        3 * flops,
        scratch=keep(3),
    )
    return (query_grad[None], passage_grad[None])

def solution(mesh):
    return jax.shard_map(
        body,
        mesh=mesh,
        in_specs=(
            P("pa", "pb", None),
            P("pa", "pb", None),
            P("pa", None),
            P("pa", None),
            P("pa", None),
        ),
        out_specs=(P("pa", "pb", None), P("pa", "pb", None)),
        check_vma=False,
    )
```

```python
import math

import jax
import jax.numpy as jnp
from jax import lax
from jax.experimental import pallas as pl
from jax.experimental.pallas import tpu as pltpu
from jax.sharding import PartitionSpec as P

F32 = jnp.float32
BF16 = jnp.bfloat16
WINDOW = 7
LAST = WINDOW - 1

def group_shift(i, step, count):
    return (i + step + count) % count

def relay_tables(count):
    every = range(count)
    return {
        "x": [(i, i ^ 1) for i in every],
        "y": [(i, i ^ 2) for i in every],
        "d": [(i, i ^ 3) for i in every],
        "za": [(i, group_shift(i, -4 if i & 2 else 4, count)) for i in every],
        "zb": [(i, group_shift(i, -4 if i & 1 else 4, count)) for i in every],
        "up": [(i, group_shift(i, 4, count)) for i in every],
        "down": [(i, group_shift(i, -4, count)) for i in every],
    }

def window_ids(i, count):
    to_y = jnp.where((i & 2) != 0, 4, -4)
    to_x = jnp.where((i & 1) != 0, 4, -4)
    return [
        i,
        i ^ 1,
        i ^ 2,
        i ^ 3,
        ((i ^ 2) + to_y + count) % count,
        ((i ^ 1) + to_x + count) % count,
        ((i ^ 3) + to_y + count) % count,
    ]

def nt_dot(a, b):
    return lax.dot_general(a, b, (((1,), (1,)), ((), ())), preferred_element_type=F32)

def tn_dot(a, b):
    return lax.dot_general(a, b, (((0,), (0,)), ((), ())), preferred_element_type=F32)

def member_slice(member, rows):
    return pl.ds(pl.multiple_of(member * rows, rows), rows)

def fold(part, top, total):
    new_top = jnp.max(part, axis=0, keepdims=True)
    if top is None:
        return new_top, jnp.sum(jnp.exp(part - new_top), axis=0, keepdims=True)
    new_top = jnp.maximum(top, new_top)
    return new_top, total * jnp.exp(top - new_top) + jnp.sum(jnp.exp(part - new_top), axis=0, keepdims=True)

def joined(pairs):
    top = pairs[0][0]
    for other, _ in pairs[1:]:
        top = jnp.maximum(top, other)
    total = jnp.zeros_like(top)
    for other, part in pairs:
        total += part * jnp.exp(other - top)
    return top + jnp.log(total)

def own_kernel(count, pb, lists, w_ref, pos_ref, p_ref, *refs):
    q_refs, (s_ref, ml_ref, full_ref, own_ref, side_ref, where_ref) = refs[:pb], refs[pb:]
    rows, width = p_ref.shape
    scale = 1.0 / math.sqrt(width)
    ids = window_ids(lax.axis_index("pa"), count)
    me = lax.axis_index("pb")
    for r in range(pb):
        full_ref[member_slice((me - r + pb) % pb, rows), :] = q_refs[r][...]
    own_ref[...] = p_ref[...]
    where_ref[...] = pos_ref[...]
    side_ref[...] = jnp.zeros_like(side_ref)
    for t in range(WINDOW):
        hit = lists[0, 0] == ids[t]
        for s in range(1, lists.shape[1]):
            hit = jnp.logical_or(hit, lists[0, s] == ids[t])
        bias = jnp.where(hit, 0.0, -jnp.inf).astype(F32)
        side_ref[t : t + 1, :] = jnp.full((1, side_ref.shape[1]), bias, F32)
    lane = lax.broadcasted_iota(jnp.int32, (1, side_ref.shape[1]), 1)
    listed = jnp.full((1, side_ref.shape[1]), -1.0, F32)
    for s in range(lists.shape[1]):
        listed = jnp.where(lane == s, lists[0, s].astype(F32), listed)
    side_ref[WINDOW : WINDOW + 1, :] = listed
    side_ref[WINDOW + 1 : WINDOW + 2, :] = w_ref[...]
    part = nt_dot(own_ref[...], full_ref[...]) * scale + side_ref[0:1, :]
    s_ref[...] = part
    ml_ref[...] = jnp.zeros_like(ml_ref)
    ml_ref[0:1, :], ml_ref[1:2, :] = fold(part, None, None)

def score_parts(full_ref, side_ref, before_ref, p_refs, s_ref, first):
    rows, width = p_refs[0].shape
    scale = 1.0 / math.sqrt(width)
    before, total = before_ref[0:1, :], before_ref[1:2, :]
    top = before
    for n, p_ref in enumerate(p_refs):
        part = nt_dot(p_ref[...], full_ref[...]) * scale + side_ref[first + n : first + n + 1, :]
        s_ref[n * rows : (n + 1) * rows, :] = part
        top = jnp.maximum(top, jnp.max(part, axis=0, keepdims=True))
    total = total * jnp.exp(before - top)
    for n in range(len(p_refs)):
        total += jnp.sum(jnp.exp(s_ref[n * rows : (n + 1) * rows, :] - top), axis=0, keepdims=True)
    return top, total

def middle_kernel(full_ref, side_ref, before_ref, *refs):
    p_refs, (s_ref, ml_ref) = refs[:-2], refs[-2:]
    ml_ref[...] = jnp.zeros_like(ml_ref)
    ml_ref[0:1, :], ml_ref[1:2, :] = score_parts(full_ref, side_ref, before_ref, p_refs, s_ref, 1)

def last_kernel(pb, full_ref, side_ref, before_ref, p_ref, s_ref, stat_ref):
    top, total = score_parts(full_ref, side_ref, before_ref, [p_ref], s_ref, LAST)
    rows = p_ref.shape[0]
    pieces = []
    for value in (top, total, side_ref[WINDOW + 1 : WINDOW + 2, :]):
        pieces += [value[:, c * rows : (c + 1) * rows] for c in range(pb)]
    pieces.append(side_ref[WINDOW : WINDOW + 1, 0:rows])
    stat_ref[...] = jnp.zeros_like(stat_ref)
    stat_ref[0 : len(pieces), :] = jnp.concatenate(pieces, axis=0)

def log_totals(stats, pb):
    return joined([(stat[0:pb, :], stat[pb : 2 * pb, :]) for stat in stats])

def query_kernel(pb, so_ref, sm_ref, sl_ref, side_ref, pos_ref, *refs):
    stat_refs, p_refs, outs, coeff = refs[:pb], refs[pb : pb + WINDOW], refs[pb + WINDOW : -1], refs[-1]
    rows, width = p_refs[0].shape
    scale = 1.0 / math.sqrt(width)
    me = lax.axis_index("pb")
    lse_rows = log_totals([ref[0] for ref in stat_refs], pb)
    lse = jnp.concatenate([lse_rows[c : c + 1, :] for c in range(pb)], axis=1)
    w = side_ref[WINDOW + 1 : WINDOW + 2, :]
    row = lax.broadcasted_iota(jnp.int32, (rows, w.shape[1]), 0)
    for t in range(WINDOW):
        if t == 0:
            prob = jnp.exp(so_ref[...] - lse) - (row == pos_ref[...] - me * rows).astype(F32)
        elif t == LAST:
            prob = jnp.exp(sl_ref[...] - lse)
        else:
            prob = jnp.exp(sm_ref[(t - 1) * rows : t * rows, :] - lse)
        coeff[t * rows : (t + 1) * rows, :] = (w * prob * scale).astype(BF16)
    for r in range(pb):
        lanes = member_slice((me + r) % pb, rows)
        total = None
        for t in range(WINDOW):
            part = tn_dot(coeff[t * rows : (t + 1) * rows, lanes], p_refs[t][...])
            total = part if total is None else total + part
        outs[r][...] = total.astype(outs[r].dtype)

def add_blocks(pb, stats, scores, pieces, orders, keep, corrections, total):
    lse_ref, weight_ref = keep
    home = lax.axis_index("pa").astype(F32)
    rows, width = pieces[0].shape
    scale = 1.0 / math.sqrt(width)
    for t, mine in enumerate(stats):
        lse_ref[t] = log_totals(mine, pb)
        weight_ref[t] = mine[0][2 * pb : 3 * pb, :]
        hit = jnp.max(jnp.where(mine[0][3 * pb : 3 * pb + 1, :] == home, 1.0, 0.0), axis=1, keepdims=True) > 0.5
        for r in range(pb):
            n = t * pb + r
            member = pl.ds(orders[n], 1)
            prob = jnp.exp(scores(n) - lse_ref[t, member, :])
            if n in corrections:
                prob = prob - corrections[n]
            value = jnp.where(hit, weight_ref[t, member, :] * prob * scale, 0.0).astype(BF16)
            part = jnp.dot(value, pieces[n][...], preferred_element_type=F32)
            total = part if total is None else total + part
    return total

def near_kernel(pb, p_ref, pos_ref, *refs):
    stat_refs, q_refs = refs[:pb], refs[pb : -4]
    out_ref, s_ref, keep = refs[-4], refs[-3], refs[-2:]
    rows, width = p_ref.shape
    scale = 1.0 / math.sqrt(width)
    me = lax.axis_index("pb")
    row = lax.broadcasted_iota(jnp.int32, (rows, rows), 0)
    full_ref = q_refs[0]
    pieces = [full_ref.at[r * rows : (r + 1) * rows, :] for r in range(pb)] + list(q_refs[1:])
    orders = list(range(pb)) + [(me - r + pb) % pb for _ in range(3) for r in range(pb)]
    corrections = {
        r: (row == pos_ref[:, r * rows : (r + 1) * rows] - me * rows).astype(F32) for r in range(pb)
    }
    for n, piece in enumerate(pieces):
        s_ref[:, n * rows : (n + 1) * rows] = nt_dot(p_ref[...], piece[...]) * scale
    stats = [[ref[t] for ref in stat_refs] for t in range(4)]
    out_ref[...] = add_blocks(
        pb, stats, lambda n: s_ref[:, n * rows : (n + 1) * rows], pieces, orders, keep, corrections, None
    )

def cross_kernel(p_ref, *refs):
    q_refs, s_ref = refs[:-1], refs[-1]
    rows, width = p_ref.shape
    scale = 1.0 / math.sqrt(width)
    for n, q_ref in enumerate(q_refs):
        s_ref[:, n * rows : (n + 1) * rows] = nt_dot(p_ref[...], q_ref[...]) * scale

def far_kernel(pb, s_ref, near_ref, *refs):
    grad_refs, up, down = refs[:pb], refs[pb : 2 * pb], refs[2 * pb : 3 * pb]
    q_refs, (out_ref, query_ref), keep = refs[3 * pb : 6 * pb], refs[6 * pb : 6 * pb + 2], refs[6 * pb + 2 :]
    rows = out_ref.shape[0]
    home, me = lax.axis_index("pa"), lax.axis_index("pb")
    y_low, x_low = (home & 2) == 0, (home & 1) == 0
    stats = []
    for k, low in ((2, y_low), (1, x_low), (3, y_low)):
        stats.append([jnp.where(low, up[c][k], down[c][k]) for c in range(pb)])
    orders = [(me - r + pb) % pb for _ in range(3) for r in range(pb)]
    out_ref[...] = add_blocks(
        pb, stats, lambda n: s_ref[:, n * rows : (n + 1) * rows], q_refs, orders, keep, {}, near_ref[...]
    )
    grad = grad_refs[0][...]
    for ref in grad_refs[1:]:
        grad = grad + ref[...].astype(F32)
    query_ref[...] = grad

VMEM = pl.BlockSpec(memory_space=pltpu.VMEM)
SMEM = pl.BlockSpec(memory_space=pltpu.SMEM)

def call(kernel, outs, args, flops, smem=0, scratch=()):
    return pl.pallas_call(
        kernel,
        out_shape=outs,
        in_specs=[SMEM] * smem + [VMEM] * (len(args) - smem),
        out_specs=[VMEM] * len(outs),
        scratch_shapes=list(scratch),
        cost_estimate=pl.CostEstimate(flops=0, bytes_accessed=0, transcendentals=0),
        compiler_params=pltpu.CompilerParams(vmem_limit_bytes=24 * 1024 * 1024),
    )(*args)

def shape(dims, dtype):
    return jax.ShapeDtypeStruct(dims, dtype)

def after(value, *others):
    return lax.optimization_barrier((value, *others))[0]

def body(queries, passages, neighbor_lists, positives, weights):
    pb, count = lax.axis_size("pb"), lax.axis_size("pa")
    rows, width = passages.shape[1:]
    q_rows = rows * pb
    tables = relay_tables(count)
    flops = 2 * rows * q_rows * width

    def move(value, name):
        return lax.ppermute(value, "pa", tables[name])

    def from_member(value, r):
        return lax.ppermute(value, "pb", [(i, (i + r) % pb) for i in range(pb)])

    def others(value):
        return [from_member(value, r) for r in range(1, pb)]

    yp, xp = move(passages[0], "y"), move(passages[0], "x")
    yq, xq = move(queries[0], "y"), move(queries[0], "x")
    own_score, own_ml, full_q, own_p, side, where = call(
        lambda *refs: own_kernel(count, pb, *refs),
        [
            shape((rows, q_rows), F32),
            shape((8, q_rows), F32),
            shape((q_rows, width), BF16),
            shape((rows, width), BF16),
            shape((16, q_rows), F32),
            shape((1, q_rows), jnp.int32),
        ],
        [neighbor_lists, weights, positives, passages[0], queries[0], *others(queries[0])],
        flops,
        smem=1,
    )
    xqs, yqs = [xq, *others(xq)], [yq, *others(yq)]
    zap, dp = move(yp, "za"), move(xp, "y")
    zbp = move(xp, "zb")
    xzp = move(after(zap, xq, yq, own_ml), "x")
    middle, middle_ml = call(
        middle_kernel,
        [shape(((LAST - 1) * rows, q_rows), F32), shape((8, q_rows), F32)],
        [full_q, side, after(own_ml, *xqs, *yqs), xp, yp, dp, zap, zbp],
        (LAST - 1) * flops,
    )
    zaq = move(after(yq, zbp), "za")
    zbq = move(after(xq, zbp), "zb")
    dq = move(after(xq, xzp), "y")
    stat_rows = -(-(3 * pb + 1) // 8) * 8
    last, stat = call(
        lambda *refs: last_kernel(pb, *refs),
        [shape((rows, q_rows), F32), shape((stat_rows, rows), F32)],
        [full_q, side, middle_ml, xzp],
        flops,
    )
    stat_x = move(stat, "x")
    stat_y = move(stat, "y")
    stat_d = move(stat_y, "x")
    four = jnp.stack([stat, stat_x, stat_y, stat_d])
    xzq = move(after(zaq, four, zbq), "x")
    up, down = move(four, "up"), move(four, "down")
    fours = [four, *others(four)]
    parts = call(
        lambda *refs: query_kernel(pb, *refs),
        [shape((rows, width), F32)] + [shape((rows, width), BF16)] * (pb - 1),
        [own_score, middle, last, side, where, *fours, own_p, xp, yp, dp, zap, zbp, xzp],
        WINDOW * flops,
        scratch=[pltpu.VMEM((WINDOW * rows, q_rows), BF16)],
    )
    arrived = [from_member(parts[r], r) for r in range(1, pb)]

    def keep(blocks):
        return [pltpu.VMEM((blocks, pb, rows), F32)] * 2

    (near,) = call(
        lambda *refs: near_kernel(pb, *refs),
        [shape((rows, width), F32)],
        [own_p, where, *fours, full_q, *xqs, *yqs, dq, *others(after(dq, parts[0]))],
        8 * flops,
        scratch=[pltpu.VMEM((rows, 4 * q_rows), F32), *keep(4)],
    )
    far_q = [zaq, *others(after(zaq, dq)), zbq, *others(after(zbq, dq)), xzq, *others(xzq)]
    (cross,) = call(cross_kernel, [shape((rows, 3 * q_rows), F32)], [own_p, *far_q], 3 * flops)
    passage_grad, query_grad = call(
        lambda *refs: far_kernel(pb, *refs),
        [shape((rows, width), F32)] * 2,
        [cross, near, parts[0], *arrived, up, *others(up), down, *others(down), *far_q],
        3 * flops,
        scratch=keep(3),
    )
    return (query_grad[None], passage_grad[None])

def solution(mesh):
    return jax.shard_map(
        body,
        mesh=mesh,
        in_specs=(
            P("pa", "pb", None),
            P("pa", "pb", None),
            P("pa", None),
            P("pa", None),
            P("pa", None),
        ),
        out_specs=(P("pa", "pb", None), P("pa", "pb", None)),
        check_vma=False,
    )
```

```python
import math

import jax
import jax.numpy as jnp
from jax import lax
from jax.experimental import pallas as pl
from jax.experimental.pallas import tpu as pltpu
from jax.sharding import PartitionSpec as P

F32 = jnp.float32
BF16 = jnp.bfloat16
WINDOW = 7
LAST = WINDOW - 1

def group_shift(i, step, count):
    return (i + step + count) % count

def relay_tables(count):
    every = range(count)
    return {
        "x": [(i, i ^ 1) for i in every],
        "y": [(i, i ^ 2) for i in every],
        "d": [(i, i ^ 3) for i in every],
        "za": [(i, group_shift(i, -4 if i & 2 else 4, count)) for i in every],
        "zb": [(i, group_shift(i, -4 if i & 1 else 4, count)) for i in every],
        "up": [(i, group_shift(i, 4, count)) for i in every],
        "down": [(i, group_shift(i, -4, count)) for i in every],
    }

def window_ids(i, count):
    to_y = jnp.where((i & 2) != 0, 4, -4)
    to_x = jnp.where((i & 1) != 0, 4, -4)
    return [
        i,
        i ^ 1,
        i ^ 2,
        i ^ 3,
        ((i ^ 2) + to_y + count) % count,
        ((i ^ 1) + to_x + count) % count,
        ((i ^ 3) + to_y + count) % count,
    ]

def nt_dot(a, b):
    return lax.dot_general(a, b, (((1,), (1,)), ((), ())), preferred_element_type=F32)

def tn_dot(a, b):
    return lax.dot_general(a, b, (((0,), (0,)), ((), ())), preferred_element_type=F32)

def member_slice(member, rows):
    return pl.ds(pl.multiple_of(member * rows, rows), rows)

def fold(part, top, total):
    new_top = jnp.max(part, axis=0, keepdims=True)
    if top is None:
        return new_top, jnp.sum(jnp.exp(part - new_top), axis=0, keepdims=True)
    new_top = jnp.maximum(top, new_top)
    return new_top, total * jnp.exp(top - new_top) + jnp.sum(jnp.exp(part - new_top), axis=0, keepdims=True)

def joined(pairs):
    top = pairs[0][0]
    for other, _ in pairs[1:]:
        top = jnp.maximum(top, other)
    total = jnp.zeros_like(top)
    for other, part in pairs:
        total += part * jnp.exp(other - top)
    return top + jnp.log(total)

def own_kernel(count, pb, lists, w_ref, pos_ref, p_ref, *refs):
    q_refs, (s_ref, ml_ref, full_ref, own_ref, side_ref, where_ref) = refs[:pb], refs[pb:]
    rows, width = p_ref.shape
    scale = 1.0 / math.sqrt(width)
    ids = window_ids(lax.axis_index("pa"), count)
    me = lax.axis_index("pb")
    for r in range(pb):
        full_ref[member_slice((me - r + pb) % pb, rows), :] = q_refs[r][...]
    own_ref[...] = p_ref[...]
    where_ref[...] = pos_ref[...]
    side_ref[...] = jnp.zeros_like(side_ref)
    for t in range(WINDOW):
        hit = lists[0, 0] == ids[t]
        for s in range(1, lists.shape[1]):
            hit = jnp.logical_or(hit, lists[0, s] == ids[t])
        bias = jnp.where(hit, 0.0, -jnp.inf).astype(F32)
        side_ref[t : t + 1, :] = jnp.full((1, side_ref.shape[1]), bias, F32)
    lane = lax.broadcasted_iota(jnp.int32, (1, side_ref.shape[1]), 1)
    listed = jnp.full((1, side_ref.shape[1]), -1.0, F32)
    for s in range(lists.shape[1]):
        listed = jnp.where(lane == s, lists[0, s].astype(F32), listed)
    side_ref[WINDOW : WINDOW + 1, :] = listed
    side_ref[WINDOW + 1 : WINDOW + 2, :] = w_ref[...]
    part = nt_dot(own_ref[...], full_ref[...]) * scale + side_ref[0:1, :]
    s_ref[...] = part
    ml_ref[...] = jnp.zeros_like(ml_ref)
    ml_ref[0:1, :], ml_ref[1:2, :] = fold(part, None, None)

def score_parts(full_ref, side_ref, before_ref, p_refs, s_ref, first):
    rows, width = p_refs[0].shape
    scale = 1.0 / math.sqrt(width)
    before, total = before_ref[0:1, :], before_ref[1:2, :]
    top = before
    for n, p_ref in enumerate(p_refs):
        part = nt_dot(p_ref[...], full_ref[...]) * scale + side_ref[first + n : first + n + 1, :]
        s_ref[n * rows : (n + 1) * rows, :] = part
        top = jnp.maximum(top, jnp.max(part, axis=0, keepdims=True))
    total = total * jnp.exp(before - top)
    for n in range(len(p_refs)):
        total += jnp.sum(jnp.exp(s_ref[n * rows : (n + 1) * rows, :] - top), axis=0, keepdims=True)
    return top, total

def middle_kernel(full_ref, side_ref, before_ref, *refs):
    p_refs, (s_ref, ml_ref) = refs[:-2], refs[-2:]
    ml_ref[...] = jnp.zeros_like(ml_ref)
    ml_ref[0:1, :], ml_ref[1:2, :] = score_parts(full_ref, side_ref, before_ref, p_refs, s_ref, 1)

def last_kernel(pb, full_ref, side_ref, before_ref, p_ref, s_ref, stat_ref):
    top, total = score_parts(full_ref, side_ref, before_ref, [p_ref], s_ref, LAST)
    rows = p_ref.shape[0]
    pieces = []
    for value in (top, total, side_ref[WINDOW + 1 : WINDOW + 2, :]):
        pieces += [value[:, c * rows : (c + 1) * rows] for c in range(pb)]
    pieces.append(side_ref[WINDOW : WINDOW + 1, 0:rows])
    stat_ref[...] = jnp.zeros_like(stat_ref)
    stat_ref[0 : len(pieces), :] = jnp.concatenate(pieces, axis=0)

def log_totals(stats, pb):
    return joined([(stat[0:pb, :], stat[pb : 2 * pb, :]) for stat in stats])

def query_kernel(pb, so_ref, sm_ref, sl_ref, side_ref, pos_ref, *refs):
    stat_refs, p_refs, outs, coeff = refs[:pb], refs[pb : pb + WINDOW], refs[pb + WINDOW : -1], refs[-1]
    rows, width = p_refs[0].shape
    scale = 1.0 / math.sqrt(width)
    me = lax.axis_index("pb")
    lse_rows = log_totals([ref[0] for ref in stat_refs], pb)
    lse = jnp.concatenate([lse_rows[c : c + 1, :] for c in range(pb)], axis=1)
    w = side_ref[WINDOW + 1 : WINDOW + 2, :]
    row = lax.broadcasted_iota(jnp.int32, (rows, w.shape[1]), 0)
    for t in range(WINDOW):
        if t == 0:
            prob = jnp.exp(so_ref[...] - lse) - (row == pos_ref[...] - me * rows).astype(F32)
        elif t == LAST:
            prob = jnp.exp(sl_ref[...] - lse)
        else:
            prob = jnp.exp(sm_ref[(t - 1) * rows : t * rows, :] - lse)
        coeff[t * rows : (t + 1) * rows, :] = (w * prob * scale).astype(BF16)
    for r in range(pb):
        lanes = member_slice((me + r) % pb, rows)
        total = None
        for t in range(WINDOW):
            part = tn_dot(coeff[t * rows : (t + 1) * rows, lanes], p_refs[t][...])
            total = part if total is None else total + part
        outs[r][...] = total.astype(outs[r].dtype)

def add_blocks(pb, stats, scores, pieces, orders, keep, corrections, total):
    lse_ref, weight_ref = keep
    home = lax.axis_index("pa").astype(F32)
    rows, width = pieces[0].shape
    scale = 1.0 / math.sqrt(width)
    for t, mine in enumerate(stats):
        lse_ref[t] = log_totals(mine, pb)
        weight_ref[t] = mine[0][2 * pb : 3 * pb, :]
        hit = jnp.max(jnp.where(mine[0][3 * pb : 3 * pb + 1, :] == home, 1.0, 0.0), axis=1, keepdims=True) > 0.5
        for r in range(pb):
            n = t * pb + r
            member = pl.ds(orders[n], 1)
            prob = jnp.exp(scores(n) - lse_ref[t, member, :])
            if n in corrections:
                prob = prob - corrections[n]
            value = jnp.where(hit, weight_ref[t, member, :] * prob * scale, 0.0).astype(BF16)
            part = jnp.dot(value, pieces[n][...], preferred_element_type=F32)
            total = part if total is None else total + part
    return total

def near_kernel(pb, p_ref, pos_ref, *refs):
    stat_refs, q_refs = refs[:pb], refs[pb : -4]
    out_ref, s_ref, keep = refs[-4], refs[-3], refs[-2:]
    rows, width = p_ref.shape
    scale = 1.0 / math.sqrt(width)
    me = lax.axis_index("pb")
    row = lax.broadcasted_iota(jnp.int32, (rows, rows), 0)
    full_ref = q_refs[0]
    pieces = [full_ref.at[r * rows : (r + 1) * rows, :] for r in range(pb)] + list(q_refs[1:])
    orders = list(range(pb)) + [(me - r + pb) % pb for _ in range(3) for r in range(pb)]
    corrections = {
        r: (row == pos_ref[:, r * rows : (r + 1) * rows] - me * rows).astype(F32) for r in range(pb)
    }
    for n, piece in enumerate(pieces):
        s_ref[:, n * rows : (n + 1) * rows] = nt_dot(p_ref[...], piece[...]) * scale
    stats = [[ref[t] for ref in stat_refs] for t in range(4)]
    out_ref[...] = add_blocks(
        pb, stats, lambda n: s_ref[:, n * rows : (n + 1) * rows], pieces, orders, keep, corrections, None
    )

def cross_kernel(p_ref, *refs):
    q_refs, s_ref = refs[:-1], refs[-1]
    rows, width = p_ref.shape
    scale = 1.0 / math.sqrt(width)
    for n, q_ref in enumerate(q_refs):
        s_ref[:, n * rows : (n + 1) * rows] = nt_dot(p_ref[...], q_ref[...]) * scale

def far_kernel(pb, s_ref, near_ref, *refs):
    grad_refs, up, down = refs[:pb], refs[pb : 2 * pb], refs[2 * pb : 3 * pb]
    q_refs, (out_hbm, query_hbm), refs = refs[3 * pb : 6 * pb], refs[6 * pb : 6 * pb + 2], refs[6 * pb + 2 :]
    keep, (out_ref, query_ref, sems) = refs[:2], refs[2:]
    rows = out_ref.shape[0]
    grad = grad_refs[0][...]
    for ref in grad_refs[1:]:
        grad = grad + ref[...].astype(F32)
    query_ref[...] = grad
    first = pltpu.make_async_copy(query_ref, query_hbm, sems.at[0])
    first.start()
    home, me = lax.axis_index("pa"), lax.axis_index("pb")
    y_low, x_low = (home & 2) == 0, (home & 1) == 0
    stats = []
    for k, low in ((2, y_low), (1, x_low), (3, y_low)):
        stats.append([jnp.where(low, up[c][k], down[c][k]) for c in range(pb)])
    orders = [(me - r + pb) % pb for _ in range(3) for r in range(pb)]
    half = rows // 2
    copies = [first]
    for h in range(2):
        part = slice(h * half, (h + 1) * half)
        out_ref[part, :] = add_blocks(
            pb, stats, lambda n: s_ref[part, n * rows : (n + 1) * rows], q_refs, orders, keep, {}, near_ref[part, :]
        )
        copy = pltpu.make_async_copy(out_ref.at[part, :], out_hbm.at[part, :], sems.at[1 + h])
        copy.start()
        copies.append(copy)
    for copy in copies:
        copy.wait()

VMEM = pl.BlockSpec(memory_space=pltpu.VMEM)
SMEM = pl.BlockSpec(memory_space=pltpu.SMEM)

def call(kernel, outs, args, flops, smem=0, scratch=(), placed=VMEM):
    return pl.pallas_call(
        kernel,
        out_shape=outs,
        in_specs=[SMEM] * smem + [VMEM] * (len(args) - smem),
        out_specs=[placed] * len(outs),
        scratch_shapes=list(scratch),
        cost_estimate=pl.CostEstimate(flops=0, bytes_accessed=0, transcendentals=0),
        compiler_params=pltpu.CompilerParams(vmem_limit_bytes=24 * 1024 * 1024),
    )(*args)

def shape(dims, dtype):
    return jax.ShapeDtypeStruct(dims, dtype)

def after(value, *others):
    return lax.optimization_barrier((value, *others))[0]

def body(queries, passages, neighbor_lists, positives, weights):
    pb, count = lax.axis_size("pb"), lax.axis_size("pa")
    rows, width = passages.shape[1:]
    q_rows = rows * pb
    tables = relay_tables(count)
    flops = 2 * rows * q_rows * width

    def move(value, name):
        return lax.ppermute(value, "pa", tables[name])

    def from_member(value, r):
        return lax.ppermute(value, "pb", [(i, (i + r) % pb) for i in range(pb)])

    def others(value):
        return [from_member(value, r) for r in range(1, pb)]

    yp, xp = move(passages[0], "y"), move(passages[0], "x")
    yq, xq = move(queries[0], "y"), move(queries[0], "x")
    own_score, own_ml, full_q, own_p, side, where = call(
        lambda *refs: own_kernel(count, pb, *refs),
        [
            shape((rows, q_rows), F32),
            shape((8, q_rows), F32),
            shape((q_rows, width), BF16),
            shape((rows, width), BF16),
            shape((16, q_rows), F32),
            shape((1, q_rows), jnp.int32),
        ],
        [neighbor_lists, weights, positives, passages[0], queries[0], *others(queries[0])],
        flops,
        smem=1,
    )
    xqs, yqs = [xq, *others(xq)], [yq, *others(yq)]
    zap, dp = move(yp, "za"), move(xp, "y")
    zbp = move(xp, "zb")
    xzp = move(after(zap, xq, yq, own_ml), "x")
    middle, middle_ml = call(
        middle_kernel,
        [shape(((LAST - 1) * rows, q_rows), F32), shape((8, q_rows), F32)],
        [full_q, side, after(own_ml, *xqs, *yqs), xp, yp, dp, zap, zbp],
        (LAST - 1) * flops,
    )
    zaq = move(after(yq, zbp), "za")
    zbq = move(after(xq, zbp), "zb")
    dq = move(after(xq, xzp), "y")
    stat_rows = -(-(3 * pb + 1) // 8) * 8
    last, stat = call(
        lambda *refs: last_kernel(pb, *refs),
        [shape((rows, q_rows), F32), shape((stat_rows, rows), F32)],
        [full_q, side, middle_ml, xzp],
        flops,
    )
    stat_x = move(stat, "x")
    stat_y = move(stat, "y")
    stat_d = move(stat_y, "x")
    four = jnp.stack([stat, stat_x, stat_y, stat_d])
    xzq = move(after(zaq, four, zbq), "x")
    up, down = move(four, "up"), move(four, "down")
    fours = [four, *others(four)]
    parts = call(
        lambda *refs: query_kernel(pb, *refs),
        [shape((rows, width), F32)] + [shape((rows, width), BF16)] * (pb - 1),
        [own_score, middle, last, side, where, *fours, own_p, xp, yp, dp, zap, zbp, xzp],
        WINDOW * flops,
        scratch=[pltpu.VMEM((WINDOW * rows, q_rows), BF16)],
    )
    arrived = [from_member(parts[r], r) for r in range(1, pb)]

    def keep(blocks):
        return [pltpu.VMEM((blocks, pb, rows), F32)] * 2

    (near,) = call(
        lambda *refs: near_kernel(pb, *refs),
        [shape((rows, width), F32)],
        [own_p, where, *fours, full_q, *xqs, *yqs, dq, *others(after(dq, parts[0]))],
        8 * flops,
        scratch=[pltpu.VMEM((rows, 4 * q_rows), F32), *keep(4)],
    )
    far_q = [zaq, *others(after(zaq, dq)), zbq, *others(after(zbq, dq)), xzq, *others(xzq)]
    (cross,) = call(cross_kernel, [shape((rows, 3 * q_rows), F32)], [own_p, *far_q], 3 * flops)
    passage_grad, query_grad = call(
        lambda *refs: far_kernel(pb, *refs),
        [shape((rows, width), F32)] * 2,
        [cross, near, parts[0], *arrived, up, *others(up), down, *others(down), *far_q],
        3 * flops,
        scratch=[
            *keep(3),
            pltpu.VMEM((rows, width), F32),
            pltpu.VMEM((rows, width), F32),
            pltpu.SemaphoreType.DMA((3,)),
        ],
        placed=pl.BlockSpec(memory_space=pl.ANY),
    )
    return (query_grad[None], passage_grad[None])

def solution(mesh):
    return jax.shard_map(
        body,
        mesh=mesh,
        in_specs=(
            P("pa", "pb", None),
            P("pa", "pb", None),
            P("pa", None),
            P("pa", None),
            P("pa", None),
        ),
        out_specs=(P("pa", "pb", None), P("pa", "pb", None)),
        check_vma=False,
    )
```
